32 devices in a mesh: slab: 8 (over z, y), subj: 2 (over core), tm: 2 (over x).
Axes of the slice: x: 2, y: 2, z: 4, core: 2. Of those that a mesh axis runs over, the one named last changes fastest.
Arguments:
- subject_data: bfloat16 [2, 16, 128, 2048], P('subj', 'slab', None, 'tm'), may hold values from -8 to 8
- template: bfloat16 [16, 128, 2048], P('slab', None, 'tm'), may hold values from -8 to 8
- neighbours: int32 [16, 27], P('slab'), may hold values from 0 to 15, as said below
- valid: int32 [16, 27], P('slab'), may hold values from 0 to 1, as said below
Outputs:
- new_template: bfloat16 [16, 128, 2048], P('slab', None, 'tm')
The draws below stay inside these ranges and needn't reach their ends.
Inputs may be any that keep to these rules, and one draw needn't show every extreme that they name: `neighbours`: slots 9 l to 9 l + 8 of block b name blocks of the slab of b shifted by l - 1 (slabs hold 2 consecutive blocks); where that slab doesn't exist they name b itself. Slot 13 names b itself. `valid`: slot 13 is always 1; slots whose slab doesn't exist are 0.
All inputs are finite; a program needn't handle non-finite values.
Results may differ from the reference program's by a relative error of at most 0.007.
Values may be sent and summed in bfloat16 or wider, within the bound.
No kernel may reach another device: no remote copies, remote signals or barrier semaphores. Data moves between devices by JAX's collectives and lax.ppermute only.
A program may use at most 64 MiB of HBM per device.

```python
import jax
import jax.numpy as jnp
from jax import lax

VB = 128
NB = 27
TIMES = 2048
ITERS = 3
BLK_DEV = 2
BLOCKS = 16
SUBJECTS = 2


def base_signal(key):
    signal_key = jax.random.fold_in(key, 11)
    return jax.random.normal(signal_key, (BLOCKS, VB, TIMES), jnp.float32)


def draw_template(key, part):
    signal = base_signal(key)
    return jnp.clip(signal, -8.0, 8.0).astype(jnp.bfloat16)


def draw_subject_data(key, part):
    signal = base_signal(key)[None]
    strength = jax.random.uniform(jax.random.fold_in(key, 12), (1, BLOCKS, VB, 1), jnp.float32, 0.05, 0.3)
    noise_key = jax.random.fold_in(key, 14)
    shape = (SUBJECTS, BLOCKS, VB, TIMES)
    noise = jax.random.normal(noise_key, shape, jnp.float32)
    mixed = strength * signal + jnp.sqrt(1.0 - strength * strength) * noise
    return jnp.clip(mixed, -8.0, 8.0).astype(jnp.bfloat16)


def neighbour_table(key):
    blocks = jnp.arange(BLOCKS, dtype=jnp.int32)[:, None]
    slot = jnp.arange(NB, dtype=jnp.int32)[None, :]
    slabs = BLOCKS // BLK_DEV
    target = blocks // BLK_DEV + slot // (NB // 3) - 1
    offset = jax.random.randint(jax.random.fold_in(key, 21), (BLOCKS, NB), 0, BLK_DEV, dtype=jnp.int32)
    present = (target >= 0) & (target < slabs)
    centre = slot == NB // 2
    named = jnp.where(present, target * BLK_DEV + offset, blocks)
    named = jnp.where(centre, blocks, named)
    keep = jax.random.randint(jax.random.fold_in(key, 22), (BLOCKS, NB), 0, 4, dtype=jnp.int32) > 0
    flag = jnp.where(centre, 1, jnp.where(present & keep, 1, 0))
    return (named.astype(jnp.int32), flag.astype(jnp.int32))


def draw_neighbours(key, part):
    return neighbour_table(key)[0]


def draw_valid(key, part):
    return neighbour_table(key)[1]


def setup_inputs(seed: int = 0) -> dict:
    key_of = jax.random.split(jax.random.key(seed), 5)
    return {
        "subject_data": draw_subject_data(jax.random.fold_in(key_of[4], 71), 0),
        "template": draw_template(jax.random.fold_in(key_of[4], 71), 0),
        "neighbours": draw_neighbours(jax.random.fold_in(key_of[4], 71), 0),
        "valid": draw_valid(jax.random.fold_in(key_of[4], 71), 0),
    }


def balance(cross, row_norm, col_norm, mask):
    width = cross.shape[-1]
    logits = cross * row_norm[None, :, None, None] * col_norm[:, None, :, :] / 0.03
    masked = mask[None, None, :, None]
    kernel = jnp.exp(logits) * masked
    target = masked / (width * jnp.sum(mask))
    filler = 1.0 - masked
    col_weight = jnp.ones((cross.shape[0], 1, cross.shape[2], width), jnp.float32)
    for step in range(ITERS):
        row_weight = 1.0 / width / lax.optimization_barrier(jnp.sum(kernel * col_weight, axis=(2, 3), keepdims=True))
        col_weight = target / (lax.optimization_barrier(jnp.sum(kernel * row_weight, axis=1, keepdims=True)) + filler)
    flow = kernel * col_weight
    return (flow / lax.optimization_barrier(jnp.sum(flow, axis=(2, 3), keepdims=True))).astype(jnp.bfloat16)

def reference(subject_data, template, neighbours, valid):
    high = lax.Precision.HIGHEST
    tmpl = template.astype(jnp.float32)
    row_scale = lax.rsqrt(lax.optimization_barrier(jnp.sum(tmpl * tmpl, axis=-1)) + 1e-06)
    data = subject_data.astype(jnp.float32)
    col_scale = lax.rsqrt(lax.optimization_barrier(jnp.sum(data * data, axis=-1)) + 1e-06)

    def one_block(index):
        slots = neighbours[index].astype(jnp.int32)
        mask = valid[index].astype(jnp.float32)
        near = jnp.take(subject_data, slots, axis=1).astype(jnp.float32)
        cross = jnp.einsum('it,skjt->sikj', tmpl[index], near, precision=high)
        plan = balance(cross, row_scale[index], jnp.take(col_scale, slots, axis=1), mask)
        moved = jnp.einsum('sikj,skjt->it', plan.astype(jnp.float32), near, precision=high)
        return (moved / SUBJECTS).astype(jnp.bfloat16)
    return lax.map(one_block, jnp.arange(BLOCKS, dtype=jnp.int32))
```

```python
import functools

import jax
import jax.numpy as jnp
from jax import lax
from jax.experimental import pallas as pl
from jax.experimental.pallas import tpu as pltpu
from jax.sharding import PartitionSpec as P

ITERS = 3
PIECES = ((0, 1, 0, 8), (1, 1, 0, 4), (1, 1, 4, 4))


def cuts(blocks, times, eighths):
    parts = []
    for first, count, start, length in PIECES if eighths else ((0, blocks, 0, 8),):
        parts.append((first, count, start * times // 8, length * times // 8))
    return parts


def rows_dot(left, right):
    return lax.dot_general(
        left, right, (((1,), (1,)), ((), ())), preferred_element_type=jnp.float32
    )


def square_sums(values):
    square = values.astype(jnp.float32)
    square = square * square
    upper = square.astype(jnp.bfloat16)
    lower = (square - upper.astype(jnp.float32)).astype(jnp.bfloat16)
    ones = jnp.ones((8, values.shape[1]), jnp.bfloat16)
    return rows_dot(ones, upper) + rows_dot(ones, lower)


def two_terms(values):
    upper = values.astype(jnp.bfloat16)
    lower = (values - upper.astype(jnp.float32)).astype(jnp.bfloat16)
    return jnp.concatenate([upper, lower], axis=0)


def cross_body(parts, blocks, width, with_rows, tmpl_ref, *refs):
    pieces, (local_ref, send_ref) = refs[: len(parts)], refs[len(parts) :]
    rows = tmpl_ref.shape[0]
    sums = [None] * blocks
    norms = [None] * blocks
    for (first, count, start, length), piece in zip(parts, pieces):
        for m in range(count):
            data = piece[m * width : (m + 1) * width, :]
            part = rows_dot(tmpl_ref[:, start : start + length], data)
            norm = square_sums(data)
            b = first + m
            sums[b] = part if sums[b] is None else sums[b] + part
            norms[b] = norm if norms[b] is None else norms[b] + norm
    for b in range(blocks):
        lanes = slice(b * width, (b + 1) * width)
        local_ref[:rows, lanes] = sums[b]
        local_ref[rows : rows + 8, lanes] = norms[b]
        send_ref[:rows, lanes] = sums[b].astype(jnp.bfloat16)
        send_ref[rows : rows + 16, lanes] = two_terms(norms[b])
    if with_rows:
        norm = square_sums(tmpl_ref[...])
        local_ref[rows + 8 : rows + 16, :] = norm
        send_ref[rows + 16 : rows + 32, :] = two_terms(norm)


def cross_call(tmpl, pieces, parts, blocks, width, with_rows):
    rows, lanes = tmpl.shape[0], blocks * width
    extra = 2 if with_rows else 1
    return pl.pallas_call(
        functools.partial(cross_body, parts, blocks, width, with_rows),
        out_shape=(
            jax.ShapeDtypeStruct((rows + 8 * extra, lanes), jnp.float32),
            jax.ShapeDtypeStruct((rows + 16 * extra, lanes), jnp.bfloat16),
        ),
    )(tmpl, *pieces)


def plan_body(parts, blocks, width, n_others, count_ref, goal_ref, *refs):
    groups = 3
    refs = list(refs)
    take = lambda n: [refs.pop(0) for _ in range(n)]
    local = take(groups)
    received = [take(n_others) for _ in range(groups)]
    data = [take(len(p)) for p in parts]
    out_ref, kernel_ref, plan_ref = refs
    rows = blocks * width
    lanes = blocks * width

    def total_rows(group, start, sent):
        value = local[group][start : start + 8, :]
        for other in received[group]:
            value = value + other[sent : sent + 8, :].astype(jnp.float32)
            value = value + other[sent + 8 : sent + 16, :].astype(jnp.float32)
        return value

    row_scale = lax.rsqrt(total_rows(0, rows + 8, rows + 16) + 1e-06)
    row_scale = jnp.transpose(jnp.broadcast_to(row_scale[:1], (width, lanes)))
    for group in range(groups):
        col_scale = lax.rsqrt(total_rows(group, rows, rows) + 1e-06)[:1] / 0.03
        for b in range(blocks):
            own = slice(b * width, (b + 1) * width)
            for m in range(blocks):
                cols = slice(m * width, (m + 1) * width)
                cross = local[group][own, cols]
                for other in received[group]:
                    cross = cross + other[own, cols].astype(jnp.float32)
                e = group * blocks + m
                kernel_ref[own, e * width : (e + 1) * width] = jnp.exp(
                    cross * row_scale[own, :] * col_scale[:, cols]
                )
    members = groups * blocks

    def kernel(b, e):
        return kernel_ref[b * width : (b + 1) * width, e * width : (e + 1) * width]

    def row_sum(b, weight):
        total = kernel(b, 0) * weight[0]
        for e in range(1, members):
            total = total + kernel(b, e) * weight[e]
        return jnp.sum(total, axis=1, keepdims=True)

    weights = [
        [jnp.full((1, width), count_ref[b, e], jnp.float32) for e in range(members)]
        for b in range(blocks)
    ]
    for step in range(ITERS):
        row_weight = [1.0 / width / row_sum(b, weights[b]) for b in range(blocks)]
        weights = [
            [
                jnp.where(
                    count_ref[b, e] > 0.0,
                    (count_ref[b, e] * goal_ref[b])
                    / jnp.sum(kernel(b, e) * row_weight[b], axis=0, keepdims=True),
                    0.0,
                )
                for e in range(members)
            ]
            for b in range(blocks)
        ]
    for b in range(blocks):
        share = 1.0 / row_sum(b, weights[b])
        for e in range(members):
            plan_ref[b * width : (b + 1) * width, e * width : (e + 1) * width] = (
                kernel(b, e) * weights[b][e] * share
            ).astype(jnp.bfloat16)

    edges = {0, out_ref.shape[1]}
    for group in parts:
        for _, _, start, length in group:
            edges |= {start, start + length}
    edges = sorted(edges)
    for low, high in zip(edges, edges[1:]):
        total = None
        for group in range(groups):
            for (first, count, start, length), piece in zip(parts[group], data[group]):
                if start <= low and high <= start + length:
                    e = group * blocks + first
                    part = jnp.dot(
                        plan_ref[:, e * width : (e + count) * width],
                        piece[:, low - start : high - start],
                        preferred_element_type=jnp.float32,
                    )
                    total = part if total is None else total + part
        out_ref[:, low:high] = total.astype(out_ref.dtype)


def plan_call(counts, goal, local, received, data, parts, blocks, width):
    rows = blocks * width
    smem = pl.BlockSpec(memory_space=pltpu.SMEM)
    vmem = pl.BlockSpec(memory_space=pltpu.VMEM)
    arrays = [*local, *(r for group in received for r in group), *(d for g in data for d in g)]
    return pl.pallas_call(
        functools.partial(plan_body, parts, blocks, width, len(received[0])),
        out_shape=jax.ShapeDtypeStruct((rows, data[0][0].shape[1]), jnp.bfloat16),
        in_specs=[smem, smem] + [vmem] * len(arrays),
        out_specs=vmem,
        scratch_shapes=[
            pltpu.VMEM((rows, 3 * rows), jnp.float32),
            pltpu.VMEM((rows, 3 * rows), jnp.bfloat16),
        ],
    )(counts, goal, *arrays)


def others(value, axis):
    count = lax.axis_size(axis)
    return [
        lax.ppermute(value, axis, [(i, (i + shift) % count) for i in range(count)])
        for shift in range(1, count)
    ]


def on_device(subject_data, template, neighbours, valid):
    _, blocks, width, times = subject_data.shape
    slabs = lax.axis_size("slab")
    subjects = subject_data.shape[0] * lax.axis_size("subj")
    slab = lax.axis_index("slab")
    data = subject_data[0]
    tmpl = template.reshape(blocks * width, times)

    pairs = [(i, i ^ 1) for i in range(slabs)]
    onward = [(i, i + 2) for i in range(0, slabs - 2, 2)]
    onward += [(i, i - 2) for i in range(3, slabs, 2)]
    parts = cuts(blocks, times, True)
    whole = cuts(blocks, times, False)
    own = [data.reshape(blocks * width, times)]
    near, far = [], []
    for first, count, start, length in parts:
        piece = data[first : first + count, :, start : start + length]
        near.append(lax.ppermute(piece, "slab", pairs))
        far.append(lax.ppermute(near[-1], "slab", onward))
    flat = lambda pieces: [p.reshape(p.shape[0] * width, p.shape[2]) for p in pieces]
    near, far = flat(near), flat(far)

    ahead = 1 - 2 * (slab % 2)
    members = jnp.arange(blocks)
    places = jnp.concatenate(
        [(slab + step) * blocks + members for step in (0, ahead, -ahead)]
    )
    used = valid.astype(jnp.float32)
    hits = (neighbours[:, :, None] == places[None, None, :]).astype(jnp.float32)
    counts = jnp.sum(hits * used[:, :, None], axis=1)
    goal = 1.0 / (width * jnp.sum(used, axis=1))

    results = [
        cross_call(tmpl, pieces, cut, blocks, width, rows)
        for pieces, cut, rows in ((own, whole, True), (near, parts, False), (far, parts, False))
    ]
    local = [r[0] for r in results]
    received = [others(r[1], "tm") for r in results]
    moved = plan_call(
        counts, goal, local, received, [own, near, far], [whole, parts, parts], blocks, width
    )
    total = moved.astype(jnp.float32)
    for other in others(moved, "subj"):
        total = total + other.astype(jnp.float32)
    return (total / subjects).astype(jnp.bfloat16).reshape(template.shape)


def solution(mesh):
    placed = (
        P("subj", "slab", None, "tm"),
        P("slab", None, "tm"),
        P("slab", None),
        P("slab", None),
    )
    return jax.shard_map(
        on_device, mesh=mesh, in_specs=placed, out_specs=P("slab", None, "tm"), check_vma=False
    )
```

```python
import functools

import jax
import jax.numpy as jnp
from jax import lax
from jax.experimental import pallas as pl
from jax.experimental.pallas import tpu as pltpu
from jax.sharding import PartitionSpec as P

ITERS = 3
SCOPE = 16 * 2**20
PIECES = ((0, 1, 0, 8), (1, 1, 0, 4), (1, 1, 4, 4))


def cuts(blocks, times, eighths):
    parts = []
    for first, count, start, length in PIECES if eighths else ((0, blocks, 0, 8),):
        parts.append((first, count, start * times // 8, length * times // 8))
    return parts


def near_core(value):
    return pltpu.with_memory_space_constraint(value, pltpu.VMEM)


def rows_dot(left, right):
    return lax.dot_general(
        left, right, (((1,), (1,)), ((), ())), preferred_element_type=jnp.float32
    )


def square_sums(values):
    square = values.astype(jnp.float32)
    square = square * square
    upper = square.astype(jnp.bfloat16)
    lower = (square - upper.astype(jnp.float32)).astype(jnp.bfloat16)
    ones = jnp.ones((8, values.shape[1]), jnp.bfloat16)
    return rows_dot(ones, upper) + rows_dot(ones, lower)


def two_terms(values):
    upper = values.astype(jnp.bfloat16)
    lower = (values - upper.astype(jnp.float32)).astype(jnp.bfloat16)
    return jnp.concatenate([upper, lower], axis=0)


def cross_body(parts, blocks, width, with_rows, tmpl_ref, *refs):
    pieces, (local_ref, send_ref) = refs[: len(parts)], refs[len(parts) :]
    rows = tmpl_ref.shape[0]
    sums = [None] * blocks
    norms = [None] * blocks
    for (first, count, start, length), piece in zip(parts, pieces):
        for m in range(count):
            data = piece[m * width : (m + 1) * width, :]
            part = rows_dot(tmpl_ref[:, start : start + length], data)
            norm = square_sums(data)
            b = first + m
            sums[b] = part if sums[b] is None else sums[b] + part
            norms[b] = norm if norms[b] is None else norms[b] + norm
    for b in range(blocks):
        lanes = slice(b * width, (b + 1) * width)
        local_ref[:rows, lanes] = sums[b]
        local_ref[rows : rows + 8, lanes] = norms[b]
        send_ref[:rows, lanes] = sums[b].astype(jnp.bfloat16)
        send_ref[rows : rows + 16, lanes] = two_terms(norms[b])
    if with_rows:
        norm = square_sums(tmpl_ref[...])
        local_ref[rows + 8 : rows + 16, :] = norm
        send_ref[rows + 16 : rows + 32, :] = two_terms(norm)


def cross_call(tmpl, pieces, parts, blocks, width, with_rows):
    rows, lanes = tmpl.shape[0], blocks * width
    extra = 2 if with_rows else 1
    return pl.pallas_call(
        functools.partial(cross_body, parts, blocks, width, with_rows),
        out_shape=(
            pltpu.VMEM((rows + 8 * extra, lanes), jnp.float32),
            pltpu.VMEM((rows + 16 * extra, lanes), jnp.bfloat16),
        ),
        compiler_params=pltpu.CompilerParams(vmem_limit_bytes=SCOPE),
    )(*map(near_core, (tmpl, *pieces)))


def plan_body(parts, blocks, width, n_others, count_ref, goal_ref, *refs):
    groups = 3
    refs = list(refs)
    take = lambda n: [refs.pop(0) for _ in range(n)]
    local = take(groups)
    received = [take(n_others) for _ in range(groups)]
    data = [take(len(p)) for p in parts]
    out_ref, kernel_ref, plan_ref = refs
    rows = blocks * width
    lanes = blocks * width

    def total_rows(group, start, sent):
        value = local[group][start : start + 8, :]
        for other in received[group]:
            value = value + other[sent : sent + 8, :].astype(jnp.float32)
            value = value + other[sent + 8 : sent + 16, :].astype(jnp.float32)
        return value

    row_scale = lax.rsqrt(total_rows(0, rows + 8, rows + 16) + 1e-06)
    row_scale = jnp.transpose(jnp.broadcast_to(row_scale[:1], (width, lanes)))
    for group in range(groups):
        col_scale = lax.rsqrt(total_rows(group, rows, rows) + 1e-06)[:1] / 0.03
        for b in range(blocks):
            own = slice(b * width, (b + 1) * width)
            for m in range(blocks):
                cols = slice(m * width, (m + 1) * width)
                cross = local[group][own, cols]
                for other in received[group]:
                    cross = cross + other[own, cols].astype(jnp.float32)
                e = group * blocks + m
                kernel_ref[own, e * width : (e + 1) * width] = jnp.exp(
                    cross * row_scale[own, :] * col_scale[:, cols]
                )
    members = groups * blocks

    def kernel(b, e):
        return kernel_ref[b * width : (b + 1) * width, e * width : (e + 1) * width]

    def row_sum(b, weight):
        total = kernel(b, 0) * weight[0]
        for e in range(1, members):
            total = total + kernel(b, e) * weight[e]
        return jnp.sum(total, axis=1, keepdims=True)

    weights = [
        [jnp.full((1, width), count_ref[b, e], jnp.float32) for e in range(members)]
        for b in range(blocks)
    ]
    for step in range(ITERS):
        row_weight = [1.0 / width / row_sum(b, weights[b]) for b in range(blocks)]
        weights = [
            [
                jnp.where(
                    count_ref[b, e] > 0.0,
                    (count_ref[b, e] * goal_ref[b])
                    / jnp.sum(kernel(b, e) * row_weight[b], axis=0, keepdims=True),
                    0.0,
                )
                for e in range(members)
            ]
            for b in range(blocks)
        ]
    for b in range(blocks):
        share = 1.0 / row_sum(b, weights[b])
        for e in range(members):
            plan_ref[b * width : (b + 1) * width, e * width : (e + 1) * width] = (
                kernel(b, e) * weights[b][e] * share
            ).astype(jnp.bfloat16)

    edges = {0, out_ref.shape[1]}
    for group in parts:
        for _, _, start, length in group:
            edges |= {start, start + length}
    edges = sorted(edges)
    for low, high in zip(edges, edges[1:]):
        total = None
        for group in range(groups):
            for (first, count, start, length), piece in zip(parts[group], data[group]):
                if start <= low and high <= start + length:
                    e = group * blocks + first
                    part = jnp.dot(
                        plan_ref[:, e * width : (e + count) * width],
                        piece[:, low - start : high - start],
                        preferred_element_type=jnp.float32,
                    )
                    total = part if total is None else total + part
        out_ref[:, low:high] = total.astype(out_ref.dtype)


def plan_call(counts, goal, local, received, data, parts, blocks, width):
    rows = blocks * width
    smem = pl.BlockSpec(memory_space=pltpu.SMEM)
    vmem = pl.BlockSpec(memory_space=pltpu.VMEM)
    arrays = [*local, *(r for group in received for r in group), *(d for g in data for d in g)]
    return pl.pallas_call(
        functools.partial(plan_body, parts, blocks, width, len(received[0])),
        out_shape=pltpu.VMEM((rows, data[0][0].shape[1]), jnp.bfloat16),
        in_specs=[smem, smem] + [vmem] * len(arrays),
        out_specs=vmem,
        scratch_shapes=[
            pltpu.VMEM((rows, 3 * rows), jnp.float32),
            pltpu.VMEM((rows, 3 * rows), jnp.bfloat16),
        ],
        compiler_params=pltpu.CompilerParams(vmem_limit_bytes=SCOPE),
    )(counts, goal, *map(near_core, arrays))


def others(value, axis):
    count = lax.axis_size(axis)
    return [
        lax.ppermute(value, axis, [(i, (i + shift) % count) for i in range(count)])
        for shift in range(1, count)
    ]


def on_device(subject_data, template, neighbours, valid):
    _, blocks, width, times = subject_data.shape
    slabs = lax.axis_size("slab")
    subjects = subject_data.shape[0] * lax.axis_size("subj")
    slab = lax.axis_index("slab")
    data = subject_data[0]
    tmpl = template.reshape(blocks * width, times)

    pairs = [(i, i ^ 1) for i in range(slabs)]
    onward = [(i, i + 2) for i in range(0, slabs - 2, 2)]
    onward += [(i, i - 2) for i in range(3, slabs, 2)]
    parts = cuts(blocks, times, True)
    whole = cuts(blocks, times, False)
    own = [data.reshape(blocks * width, times)]
    near, far = [], []
    for first, count, start, length in parts:
        piece = data[first : first + count, :, start : start + length]
        near.append(lax.ppermute(piece, "slab", pairs))
        far.append(lax.ppermute(near[-1], "slab", onward))
    flat = lambda pieces: [p.reshape(p.shape[0] * width, p.shape[2]) for p in pieces]
    near, far = flat(near), flat(far)

    ahead = 1 - 2 * (slab % 2)
    members = jnp.arange(blocks)
    places = jnp.concatenate(
        [(slab + step) * blocks + members for step in (0, ahead, -ahead)]
    )
    used = valid.astype(jnp.float32)
    hits = (neighbours[:, :, None] == places[None, None, :]).astype(jnp.float32)
    counts = jnp.sum(hits * used[:, :, None], axis=1)
    goal = 1.0 / (width * jnp.sum(used, axis=1))

    results = [
        cross_call(tmpl, pieces, cut, blocks, width, rows)
        for pieces, cut, rows in ((own, whole, True), (near, parts, False), (far, parts, False))
    ]
    local = [r[0] for r in results]
    received = [others(r[1], "tm") for r in results]
    moved = plan_call(
        counts, goal, local, received, [own, near, far], [whole, parts, parts], blocks, width
    )
    total = moved.astype(jnp.float32)
    for other in others(moved, "subj"):
        total = total + other.astype(jnp.float32)
    return (total / subjects).astype(jnp.bfloat16).reshape(template.shape)


def solution(mesh):
    placed = (
        P("subj", "slab", None, "tm"),
        P("slab", None, "tm"),
        P("slab", None),
        P("slab", None),
    )
    return jax.shard_map(
        on_device, mesh=mesh, in_specs=placed, out_specs=P("slab", None, "tm"), check_vma=False
    )
```
